32 devices in a mesh: dp: 4 (over z), row: 4 (over y, core), col: 2 (over x).
Axes of the slice: x: 2, y: 2, z: 4, core: 2. Of those that a mesh axis runs over, the one named last changes fastest.
Arguments:
- tokens: bfloat16 [32, 1024, 768], P(('dp', 'row'), 'col'), may hold values from -6 to 6
- cotangent: bfloat16 [32, 1024, 768], P(('dp', 'row'), 'col'), may hold values from -6 to 6
- prefix: int32 [32], P(('dp', 'row')), may hold values from 102 to 512, as said below
- offsets: int32 [12], replicated, may hold values from 0 to 11, each once
- qkv_weight: bfloat16 [768, 2304], P('row', 'col'), may hold values from -0.21875 to 0.21875
- proj_weight: bfloat16 [768, 768], P('row', 'col'), may hold values from -0.21875 to 0.21875
- up_weight: bfloat16 [768, 3072], P('row', 'col'), may hold values from -0.21875 to 0.21875
- down_weight: bfloat16 [3072, 768], P('row', 'col'), may hold values from -0.109375 to 0.109375
- norm_gains: float32 [3, 768], replicated, may hold values from 0.5 to 1.5
- model_biases: float32 [7, 768], replicated, may hold values from -1 to 1
- hidden_gain: float32 [3072], replicated, may hold values from 0.5 to 1.5
- hidden_biases: float32 [2, 3072], replicated, may hold values from -1 to 1
Outputs:
- output: bfloat16 [32, 1024, 768], P(('dp', 'row'), 'col')
- input_grad: float32 [32, 1024, 768], P(('dp', 'row'), 'col')
- qkv_grad: float32 [768, 2304], P('row', 'col')
- proj_grad: float32 [768, 768], P('row', 'col')
- up_grad: float32 [768, 3072], P('row', 'col')
- down_grad: float32 [3072, 768], P('row', 'col')
- gains_grad: float32 [3, 768], replicated
- biases_grad: float32 [7, 768], replicated
- hidden_gain_grad: float32 [3072], replicated
- hidden_biases_grad: float32 [2, 3072], replicated
The draws below stay inside these ranges and needn't reach their ends.
Inputs may be any that keep to these rules, and one draw needn't show every extreme that they name: `prefix`: one value a sequence; some sequence has exactly 102 and some exactly 512. `offsets`: each value appears once.
All inputs are finite; a program needn't handle non-finite values.
Results may differ from the reference program's by a relative error of at most 0.018.
Values may be sent and summed in bfloat16 or wider, within the bound.
A program may use at most 256 MiB of HBM per device.

```python
import math
import jax
import jax.numpy as jnp
from jax import lax

D = 768
HEADS = 12
FF = 3072
SEQ = 1024
HEAD_DIM = 64
SEQS = 32


def draw_prefix(key, part):
    values = jax.random.randint(key, (SEQS,), SEQ // 10, SEQ // 2 + 1)
    return values.at[0].set(SEQ // 2).at[1].set(SEQ // 10)


def levels(rng, dims, shards, low, high):
    loudness, own = 1.0, jax.random.fold_in(rng, 6)
    for dim, shards_of in shards:
        draws = jnp.exp(jax.random.uniform(jax.random.fold_in(own, dim), (shards_of,), jnp.float32, low / len(shards), high / len(shards)))
        loudness = loudness * jnp.repeat(draws, dims[dim] // shards_of).reshape([-1 if axis == dim else 1 for axis in range(len(dims))])
    return loudness


def gaussian(own_key, extent, width, most, pieces=(), kind=jnp.bfloat16):
    values = jax.random.normal(own_key, extent, jnp.float32) * width
    if len(pieces) > 0:
        values = levels(own_key, extent, pieces, -0.22, 0.18) * values
    return jnp.clip(values, min=-most, max=most).astype(kind)


def setup_inputs(seed: int = 0) -> dict:
    key_list = jax.random.split(jax.random.key(seed), 13)
    tokens = gaussian(key_list[0], (SEQS, SEQ, D), 1.0, 6.0, ((0, 16), (1, 2)))
    cotangent = gaussian(key_list[1], (SEQS, SEQ, D), 1.0, 6.0, ((0, 16), (1, 2)))
    prefix = draw_prefix(jax.random.fold_in(key_list[12], 71), 0)
    offsets = jax.random.permutation(key_list[3], HEADS).astype(jnp.int32)
    qkv_weight = gaussian(key_list[4], (D, 3 * D), D ** -0.5, 0.21875, ((0, 4), (1, 2)))
    proj_weight = gaussian(key_list[5], (D, D), D ** -0.5, 0.21875, ((0, 4), (1, 2)))
    up_weight = gaussian(key_list[6], (D, FF), D ** -0.5, 0.21875, ((0, 4), (1, 2)))
    down_weight = gaussian(key_list[7], (FF, D), FF ** -0.5, 0.109375, ((0, 4), (1, 2)))
    norm_gains = jnp.clip(1.0 + 0.1 * jax.random.normal(key_list[8], (3, D), jnp.float32), 0.5, 1.5)
    model_biases = gaussian(key_list[9], (7, D), 0.2, 1.0, (), jnp.float32)
    hidden_gain = jnp.clip(1.0 + 0.1 * jax.random.normal(key_list[10], (FF,), jnp.float32), 0.5, 1.5)
    hidden_biases = gaussian(key_list[11], (2, FF), 0.2, 1.0, (), jnp.float32)
    return dict(tokens=tokens, cotangent=cotangent, prefix=prefix, offsets=offsets, qkv_weight=qkv_weight, proj_weight=proj_weight, up_weight=up_weight, down_weight=down_weight, norm_gains=norm_gains, model_biases=model_biases, hidden_gain=hidden_gain, hidden_biases=hidden_biases)


@jax.custom_vjp
def low(v):
    return lax.optimization_barrier(v.astype(jnp.bfloat16)).astype(jnp.float32)

@jax.custom_vjp
def low_back(v):
    return v

def low_keep(v):
    return (low(v), None)

def low_pass(kept, grad):
    return (grad,)

def back_keep(v):
    return (v, None)

def back_low(kept, grad):
    return (low(grad),)
low.defvjp(low_keep, low_pass)
low_back.defvjp(back_keep, back_low)
dilation_steps = (1, 2, 4, 6, 12)
eps_norm = 1e-05
masked_fill = -1e+30

def normalize(values):
    center = values - lax.optimization_barrier(jnp.mean(values, axis=-1, keepdims=True))
    return center * lax.rsqrt(lax.optimization_barrier(jnp.mean(center * center, axis=-1, keepdims=True)) + eps_norm)

def matmul(left, right):
    return jnp.dot(left, right, precision=lax.Precision.HIGHEST, preferred_element_type=jnp.float32)

def multiplicity(offsets, prefix_len):
    positions = jnp.arange(SEQ, dtype=jnp.int32)
    counts = jnp.zeros((HEADS, SEQ, SEQ), jnp.float32)
    for dilation in dilation_steps:
        hits = positions[None, :] % dilation == offsets[:, None] % dilation
        counts = counts + (hits[:, :, None] & hits[:, None, :]).astype(jnp.float32)
    visible = (positions[None, :] <= positions[:, None]) | (positions[None, :] < prefix_len)
    return jnp.where(visible[None], counts, 0.0)

def layer(inputs, weights, counts):
    qkv_w, proj_w, up_w, down_w, gains, biases, gain_hidden, biases_hidden = weights
    first_in = low(normalize(inputs) * gains[0] + biases[0])
    bias_packed = jnp.concatenate([biases[3], jnp.zeros_like(biases[3]), biases[4]])
    packed = low(low_back(matmul(first_in, qkv_w) + bias_packed))
    split_heads = packed.reshape(SEQ, 3, HEADS, HEAD_DIM)
    queries = split_heads[:, 0].transpose(1, 0, 2)
    keys_all = split_heads[:, 1].transpose(1, 0, 2)
    values_all = split_heads[:, 2].transpose(1, 0, 2)
    scores = jnp.einsum('hqd,hkd->hqk', queries, keys_all, precision=lax.Precision.HIGHEST)
    scores = low_back(scores * (1.0 / math.sqrt(HEAD_DIM)))
    logits = jnp.where(counts > 0, scores + jnp.log(jnp.maximum(counts, 1.0)), masked_fill)
    row_peak = lax.optimization_barrier(jnp.max(logits, axis=-1, keepdims=True))
    expo_terms = jnp.exp(logits - row_peak)
    probs_low = low(expo_terms / lax.optimization_barrier(jnp.sum(expo_terms, axis=-1, keepdims=True)))
    context = jnp.einsum('hqk,hkd->qhd', probs_low, values_all, precision=lax.Precision.HIGHEST)
    context = low(low_back(context.reshape(SEQ, D)))
    inner = low(normalize(context) * gains[1] + biases[1])
    branch = low_back(matmul(inner, proj_w) + biases[5])
    middle = inputs + branch
    second_in = low(normalize(middle) * gains[2] + biases[2])
    pre_act = low_back(matmul(second_in, up_w) + biases_hidden[1])
    activ = jax.nn.gelu(pre_act, approximate=False)
    inner_ff = low(normalize(activ) * gain_hidden + biases_hidden[0])
    branch_ff = low_back(matmul(inner_ff, down_w) + biases[6])
    return middle + branch_ff

def reference(tokens, cotangent, prefix, offsets, qkv_weight, proj_weight, up_weight, down_weight, norm_gains, model_biases, hidden_gain, hidden_biases):
    params = tuple((p.astype(jnp.float32) for p in (qkv_weight, proj_weight, up_weight, down_weight, norm_gains, model_biases, hidden_gain, hidden_biases)))

    def per_sequence(carry, element):
        sequence, upstream, prefix_len = element
        counts = multiplicity(offsets, prefix_len)

        def forward(inputs, *weights):
            return layer(inputs, weights, counts)
        result, pull = jax.vjp(forward, sequence.astype(jnp.float32), *params)
        grads = pull(upstream.astype(jnp.float32))
        carry = tuple((running + grad for running, grad in zip(carry, grads[1:])))
        return (carry, (result.astype(jnp.bfloat16), grads[0]))
    start = tuple((jnp.zeros_like(p) for p in params))
    sums, (outputs, input_grads) = lax.scan(per_sequence, start, (tokens, cotangent, prefix))
    return (outputs, input_grads, sums[0], sums[1], sums[2], sums[3], sums[4], sums[5], sums[6], sums[7])
```

```python
import functools
import math

import jax
import jax.numpy as jnp
import numpy as np
from jax import lax
from jax.experimental import pallas as pl
from jax.experimental.pallas import tpu as pltpu
from jax.sharding import PartitionSpec as P

HEADS = 12


dilation_steps = (1, 2, 4, 6, 12)
eps_norm = 1e-05
masked_fill = -1e30
prefix_most = 512
period = 12
log_parts = 3
q_rows = 256


def normalize_keep(values):
    center = values - jnp.mean(values, axis=-1, keepdims=True)
    rescale = lax.rsqrt(jnp.mean(center * center, axis=-1, keepdims=True) + eps_norm)
    return (center * rescale, rescale)


def norm_back(upstream, normed, rescale):
    mean_up = jnp.mean(upstream, axis=-1, keepdims=True)
    mean_cross = jnp.mean(upstream * normed, axis=-1, keepdims=True)
    return rescale * (upstream - mean_up - normed * mean_cross)


def gelu_exact(values):
    return jax.nn.gelu(values, approximate=False)


def assemble(stacked, n_row, n_col):
    tile_rows = stacked.shape[1]
    tile_cols = stacked.shape[2]
    grid = stacked.reshape(n_row, n_col, tile_rows, tile_cols).transpose(0, 2, 1, 3)
    return grid.reshape(n_row * tile_rows, n_col * tile_cols)


def grid_tiles(matrix, n_row, n_col):
    tile_rows = matrix.shape[0] // n_row
    tile_cols = matrix.shape[1] // n_col
    grid = matrix.reshape(n_row, tile_rows, n_col, tile_cols).transpose(0, 2, 1, 3)
    return grid.reshape(n_row * n_col, tile_rows, tile_cols)


def split_logs():
    logs = np.log(np.arange(1, len(dilation_steps) + 1, dtype=np.float64))
    parts = []
    for _ in range(log_parts):
        part = logs.astype(jnp.bfloat16)
        parts.append(part)
        logs = logs - part.astype(np.float64)
    return parts


def bias_tables(offsets, seq_len, head_size):
    lane = np.arange(head_size)
    used = lane < log_parts * period
    residue = lane % period
    hit = (np.arange(seq_len)[:, None] % period == residue[None]) & used[None]
    query_side = jnp.asarray(np.tile(hit, (1, 2)), jnp.bfloat16)
    ring = jnp.arange(period, dtype=jnp.int32)
    phase = offsets[:, None, None]
    counts = jnp.zeros((offsets.shape[0], period, period), jnp.int32)
    for dilation in dilation_steps:
        hit_here = (ring % dilation)[None, :, None] == phase % dilation
        counts = counts + (hit_here & hit_here.transpose(0, 2, 1)).astype(jnp.int32)
    parts = []
    for part in split_logs():
        value = jnp.zeros(counts.shape, jnp.bfloat16)
        for count in range(1, len(dilation_steps) + 1):
            value = jnp.where(counts == count, jnp.asarray(part[count - 1]), value)
        parts.append(value)
    table = jnp.stack(parts, axis=2)
    table = table.reshape(offsets.shape[0], period, log_parts * period)
    table = jnp.pad(table, ((0, 0), (0, 0), (0, head_size - log_parts * period)))
    swapped = table.reshape(-1, 2, period, head_size)[:, ::-1]
    flat = swapped.transpose(2, 0, 1, 3).reshape(period, -1)
    pick = jnp.asarray(
        np.arange(seq_len)[:, None] % period == np.arange(period)[None], jnp.bfloat16
    )
    key_side = jnp.dot(pick, flat, preferred_element_type=jnp.float32).astype(jnp.bfloat16)
    return query_side, key_side


def visible_keys(first, rows, seq_len):
    return min(seq_len, max(first + rows, prefix_most))


def mask_tile(scores, first, rows, prefix_len, fill):
    seen = scores.shape[0]
    clear = min(first, seen)
    key_pos = lax.broadcasted_iota(jnp.int32, (seen - clear, rows), 0) + clear
    query_pos = lax.broadcasted_iota(jnp.int32, (1, rows), 1) + first
    last = jnp.maximum(query_pos, prefix_len - 1)
    hidden = jnp.where(key_pos <= last, scores[clear:], fill)
    if clear == 0:
        return hidden
    return jnp.concatenate([scores[:clear], hidden], axis=0)


def attn_fwd_kernel(prefix_ref, q_ref, k_ref, v_ref, qb_ref, kb_ref, out_ref, lse_ref, turned):
    seq_len, pair_width = q_ref.shape
    head_size = pair_width // 2
    scale = jnp.bfloat16(1.0 / math.sqrt(head_size))
    prefix_len = prefix_ref[0]
    lower = lax.broadcasted_iota(jnp.int32, (seq_len, pair_width), 1) < head_size
    queries = q_ref[...] * scale
    keys_all = k_ref[...]
    values_turned = v_ref[...].T
    for half in range(2):
        own = lower if half == 0 else jnp.logical_not(lower)
        query_aug = jnp.where(own, queries, qb_ref[...])
        key_aug = jnp.where(own, keys_all, kb_ref[...])
        rows_of = slice(half * head_size, (half + 1) * head_size)
        for first in range(0, seq_len, q_rows):
            seen = visible_keys(first, q_rows, seq_len)
            scores = lax.dot_general(
                key_aug[:seen],
                query_aug[first : first + q_rows],
                (((1,), (1,)), ((), ())),
                preferred_element_type=jnp.float32,
            )
            scores = mask_tile(scores, first, q_rows, prefix_len, masked_fill)
            peak = jnp.max(scores, axis=0, keepdims=True)
            expo = jnp.exp(scores - peak)
            total = jnp.sum(expo, axis=0, keepdims=True)
            mixed = jnp.dot(
                values_turned[rows_of, :seen],
                expo.astype(jnp.bfloat16),
                preferred_element_type=jnp.float32,
            )
            turned[rows_of, first : first + q_rows] = mixed / total
            lse_ref[0, half : half + 1, first : first + q_rows] = peak + jnp.log(total)
    out_ref[...] = turned[...].T.astype(out_ref.dtype)


def attn_bwd_kernel(
    prefix_ref,
    q_ref,
    k_ref,
    v_ref,
    qb_ref,
    kb_ref,
    out_ref,
    lse_ref,
    grad_ref,
    packed_ref,
    dq_turned,
    dk_total,
    dv_total,
):
    seq_len, pair_width = q_ref.shape
    head_size = pair_width // 2
    scale = 1.0 / math.sqrt(head_size)
    prefix_len = prefix_ref[0]
    lower = lax.broadcasted_iota(jnp.int32, (seq_len, pair_width), 1) < head_size
    queries = q_ref[...] * jnp.bfloat16(scale)
    keys_all = k_ref[...]
    values_all = v_ref[...]
    grads = grad_ref[...]
    keys_turned = keys_all.T
    mixed = (grads.astype(jnp.float32) * out_ref[...].astype(jnp.float32)).T
    dk_total[...] = jnp.zeros_like(dk_total)
    dv_total[...] = jnp.zeros_like(dv_total)
    for half in range(2):
        own = lower if half == 0 else jnp.logical_not(lower)
        query_aug = jnp.where(own, queries, qb_ref[...])
        key_aug = jnp.where(own, keys_all, kb_ref[...])
        query_own = jnp.where(own, queries, jnp.bfloat16(0))
        grad_own = jnp.where(own, grads, jnp.bfloat16(0))
        rows_of = slice(half * head_size, (half + 1) * head_size)
        delta = jnp.sum(mixed[rows_of], axis=0, keepdims=True)
        for first in range(0, seq_len, q_rows):
            block = slice(first, first + q_rows)
            seen = visible_keys(first, q_rows, seq_len)
            scores = lax.dot_general(
                key_aug[:seen],
                query_aug[block],
                (((1,), (1,)), ((), ())),
                preferred_element_type=jnp.float32,
            )
            scores = scores - lse_ref[0, half : half + 1, block]
            probs = jnp.exp(mask_tile(scores, first, q_rows, prefix_len, masked_fill))
            d_prob = lax.dot_general(
                values_all[:seen],
                grad_own[block],
                (((1,), (1,)), ((), ())),
                preferred_element_type=jnp.float32,
            )
            d_score = (probs * (d_prob - delta[:, block])).astype(jnp.bfloat16)
            dv_total[:seen] += jnp.dot(
                probs.astype(jnp.bfloat16), grad_own[block], preferred_element_type=jnp.float32
            )
            dk_total[:seen] += jnp.dot(
                d_score, query_own[block], preferred_element_type=jnp.float32
            )
            dq_turned[rows_of, block] = (
                jnp.dot(
                    keys_turned[rows_of, :seen], d_score, preferred_element_type=jnp.float32
                )
                * scale
            )
    packed_ref[0] = dq_turned[...].T.astype(packed_ref.dtype)
    packed_ref[1] = dk_total[...].astype(packed_ref.dtype)
    packed_ref[2] = dv_total[...].astype(packed_ref.dtype)


def attn_specs(seq_len, pair_width, pairs):
    def part(which):
        return pl.BlockSpec((seq_len, pair_width), lambda p: (0, which * pairs + p))

    return [
        pl.BlockSpec(memory_space=pltpu.SMEM),
        part(0),
        part(1),
        part(2),
        pl.BlockSpec((seq_len, pair_width), lambda p: (0, 0)),
        pl.BlockSpec((seq_len, pair_width), lambda p: (0, p)),
    ]


def attn_fwd(packed, prefix_len, query_side, key_side):
    seq_len = packed.shape[0]
    width = packed.shape[1] // 3
    pair_width = 2 * (width // HEADS)
    pairs = HEADS // 2
    cost = pl.CostEstimate(
        flops=4 * width * seq_len * seq_len,
        bytes_accessed=10 * width * seq_len,
        transcendentals=HEADS * seq_len * seq_len,
    )
    return pl.pallas_call(
        attn_fwd_kernel,
        grid=(pairs,),
        in_specs=attn_specs(seq_len, pair_width, pairs),
        out_specs=[
            pl.BlockSpec((seq_len, pair_width), lambda p: (0, p)),
            pl.BlockSpec((1, 8, seq_len), lambda p: (p, 0, 0)),
        ],
        out_shape=[
            jax.ShapeDtypeStruct((seq_len, width), jnp.bfloat16),
            jax.ShapeDtypeStruct((pairs, 8, seq_len), jnp.float32),
        ],
        scratch_shapes=[pltpu.VMEM((pair_width, seq_len), jnp.float32)],
        cost_estimate=cost,
        name="attn_fwd",
    )(prefix_len, packed, packed, packed, query_side, key_side)


def attn_bwd(packed, prefix_len, query_side, key_side, context, lse, d_context):
    seq_len = packed.shape[0]
    width = packed.shape[1] // 3
    pair_width = 2 * (width // HEADS)
    pairs = HEADS // 2
    tile = pl.BlockSpec((seq_len, pair_width), lambda p: (0, p))
    cost = pl.CostEstimate(
        flops=10 * width * seq_len * seq_len,
        bytes_accessed=20 * width * seq_len,
        transcendentals=HEADS * seq_len * seq_len,
    )
    return pl.pallas_call(
        attn_bwd_kernel,
        grid=(pairs,),
        in_specs=attn_specs(seq_len, pair_width, pairs)
        + [tile, pl.BlockSpec((1, 8, seq_len), lambda p: (p, 0, 0)), tile],
        out_specs=pl.BlockSpec((3, seq_len, pair_width), lambda p: (0, 0, p)),
        out_shape=jax.ShapeDtypeStruct((3, seq_len, width), jnp.bfloat16),
        scratch_shapes=[
            pltpu.VMEM((pair_width, seq_len), jnp.float32),
            pltpu.VMEM((seq_len, pair_width), jnp.float32),
            pltpu.VMEM((seq_len, pair_width), jnp.float32),
        ],
        cost_estimate=cost,
        name="attn_bwd",
    )(prefix_len, packed, packed, packed, query_side, key_side, context, lse, d_context)


def swap_col(values):
    return lax.ppermute(values, "col", [(0, 1), (1, 0)])


def to_whole(pieces):
    me = lax.axis_index("col")
    kept = lax.dynamic_index_in_dim(pieces, me, 0, keepdims=False)
    arrived = swap_col(lax.dynamic_index_in_dim(pieces, 1 - me, 0, keepdims=False))
    first = jnp.where(me == 0, kept, arrived)
    second = jnp.where(me == 0, arrived, kept)
    return jnp.concatenate([first, second], axis=0)


def to_pieces(whole, link_type):
    me = lax.axis_index("col")
    half_len = whole.shape[0] // 2
    parts = whole.reshape(2, half_len, whole.shape[1])
    kept = lax.dynamic_index_in_dim(parts, me, 0, keepdims=False)
    sent = lax.dynamic_index_in_dim(parts, 1 - me, 0, keepdims=False)
    arrived = swap_col(sent.astype(link_type)).astype(whole.dtype)
    first = jnp.where(me == 0, kept, arrived)
    second = jnp.where(me == 0, arrived, kept)
    return jnp.stack([first, second])


def body(
    tokens,
    cotangent,
    prefix,
    offsets,
    qkv_weight,
    proj_weight,
    up_weight,
    down_weight,
    norm_gains,
    model_biases,
    hidden_gain,
    hidden_biases,
):
    n_row = lax.axis_size("row")
    n_col = lax.axis_size("col")
    gathered = (
        lax.all_gather(qkv_weight[None], ("row", "col"), axis=0, tiled=True),
        lax.all_gather(proj_weight[None], ("row", "col"), axis=0, tiled=True),
        lax.all_gather(up_weight[None], ("row", "col"), axis=0, tiled=True),
        lax.all_gather(down_weight[None], ("row", "col"), axis=0, tiled=True),
    )
    qkv_full, proj_full, up_full, down_full = [
        assemble(stacked, n_row, n_col) for stacked in gathered
    ]
    model_width = tokens.shape[2]
    seq_len = tokens.shape[1] * n_col
    head_size = model_width // HEADS
    prefix_len = lax.dynamic_slice_in_dim(prefix, lax.axis_index("col"), 1)
    query_side, key_side = bias_tables(offsets, seq_len, head_size)
    inputs = to_whole(tokens).astype(jnp.float32)
    cotangent_whole = to_whole(cotangent)
    normed_first, rescale_first = normalize_keep(inputs)
    first_in = (normed_first * norm_gains[0] + model_biases[0]).astype(jnp.bfloat16)
    bias_packed = jnp.concatenate(
        [model_biases[3], jnp.zeros_like(model_biases[3]), model_biases[4]]
    )
    packed = (jnp.dot(first_in, qkv_full, preferred_element_type=jnp.float32) + bias_packed).astype(
        jnp.bfloat16
    )
    context_low, lse = attn_fwd(packed, prefix_len, query_side, key_side)
    context_flat = context_low.astype(jnp.float32)
    normed_attn, rescale_attn = normalize_keep(context_flat)
    inner = (normed_attn * norm_gains[1] + model_biases[1]).astype(jnp.bfloat16)
    middle = (
        inputs + jnp.dot(inner, proj_full, preferred_element_type=jnp.float32) + model_biases[5]
    )
    normed_second, rescale_second = normalize_keep(middle)
    second_in = (normed_second * norm_gains[2] + model_biases[2]).astype(jnp.bfloat16)
    pre_act = jnp.dot(second_in, up_full, preferred_element_type=jnp.float32) + hidden_biases[1]
    activ, gelu_pull = jax.vjp(gelu_exact, pre_act)
    normed_hidden, rescale_hidden = normalize_keep(activ)
    inner_ff = (normed_hidden * hidden_gain + hidden_biases[0]).astype(jnp.bfloat16)
    result = (
        middle + jnp.dot(inner_ff, down_full, preferred_element_type=jnp.float32) + model_biases[6]
    )
    output = to_pieces(result.astype(jnp.bfloat16), jnp.bfloat16)
    up_low = cotangent_whole
    upstream = up_low.astype(jnp.float32)
    down_grad = jnp.einsum("tf,td->fd", inner_ff, up_low, preferred_element_type=jnp.float32)
    d_inner_ff = jnp.dot(up_low, down_full.T, preferred_element_type=jnp.float32)
    d_activ = norm_back(d_inner_ff * hidden_gain, normed_hidden, rescale_hidden)
    d_pre = gelu_pull(d_activ)[0].astype(jnp.bfloat16)
    up_grad = jnp.einsum("td,tf->df", second_in, d_pre, preferred_element_type=jnp.float32)
    d_second = jnp.dot(d_pre, up_full.T, preferred_element_type=jnp.float32)
    d_middle = upstream + norm_back(d_second * norm_gains[2], normed_second, rescale_second)
    d_branch = d_middle.astype(jnp.bfloat16)
    proj_grad = jnp.einsum("td,te->de", inner, d_branch, preferred_element_type=jnp.float32)
    d_inner = jnp.dot(d_branch, proj_full.T, preferred_element_type=jnp.float32)
    d_context = norm_back(d_inner * norm_gains[1], normed_attn, rescale_attn).astype(jnp.bfloat16)
    d_split = attn_bwd(packed, prefix_len, query_side, key_side, context_low, lse, d_context)
    d_packed = jnp.concatenate([d_split[0], d_split[1], d_split[2]], axis=1)
    qkv_grad = jnp.einsum("td,tf->df", first_in, d_packed, preferred_element_type=jnp.float32)
    d_first = jnp.dot(d_packed, qkv_full.T, preferred_element_type=jnp.float32)
    query_bias_sum = jnp.sum(d_split[0].astype(jnp.float32), axis=0)
    value_bias_sum = jnp.sum(d_split[2].astype(jnp.float32), axis=0)
    input_grad = to_pieces(
        d_middle + norm_back(d_first * norm_gains[0], normed_first, rescale_first), jnp.bfloat16
    )
    gains_local = jnp.stack(
        [
            jnp.sum(d_first * normed_first, axis=0),
            jnp.sum(d_inner * normed_attn, axis=0),
            jnp.sum(d_second * normed_second, axis=0),
        ]
    )
    biases_local = jnp.stack(
        [
            jnp.sum(d_first, axis=0),
            jnp.sum(d_inner, axis=0),
            jnp.sum(d_second, axis=0),
            query_bias_sum,
            value_bias_sum,
            jnp.sum(d_branch.astype(jnp.float32), axis=0),
            jnp.sum(up_low.astype(jnp.float32), axis=0),
        ]
    )
    hidden_gain_local = jnp.sum(d_inner_ff * normed_hidden, axis=0)
    hidden_biases_local = jnp.stack(
        [jnp.sum(d_inner_ff, axis=0), jnp.sum(d_pre.astype(jnp.float32), axis=0)]
    )
    gains_grad, biases_grad, hidden_gain_grad, hidden_biases_grad = lax.psum(
        (gains_local, biases_local, hidden_gain_local, hidden_biases_local), ("dp", "row", "col")
    )
    matrices = (qkv_grad, proj_grad, up_grad, down_grad)
    tiles = tuple((grid_tiles(matrix, n_row, n_col) for matrix in matrices))
    owned = (
        lax.psum_scatter(
            tiles[0].astype(jnp.bfloat16), ("row", "col"), scatter_dimension=0, tiled=True
        ).astype(jnp.float32),
        lax.psum_scatter(
            tiles[1].astype(jnp.bfloat16), ("row", "col"), scatter_dimension=0, tiled=True
        ).astype(jnp.float32),
        lax.psum_scatter(
            tiles[2].astype(jnp.bfloat16), ("row", "col"), scatter_dimension=0, tiled=True
        ).astype(jnp.float32),
        lax.psum_scatter(
            tiles[3].astype(jnp.bfloat16), ("row", "col"), scatter_dimension=0, tiled=True
        ).astype(jnp.float32),
    )
    blocks = (
        lax.psum(owned[0][0].astype(jnp.bfloat16), "dp").astype(jnp.float32),
        lax.psum(owned[1][0].astype(jnp.bfloat16), "dp").astype(jnp.float32),
        lax.psum(owned[2][0].astype(jnp.bfloat16), "dp").astype(jnp.float32),
        lax.psum(owned[3][0].astype(jnp.bfloat16), "dp").astype(jnp.float32),
    )
    return (
        output,
        input_grad,
        blocks[0],
        blocks[1],
        blocks[2],
        blocks[3],
        gains_grad,
        biases_grad,
        hidden_gain_grad,
        hidden_biases_grad,
    )


def solution(mesh):
    placed = (
        P(("dp", "row"), "col", None),
        P(("dp", "row"), "col", None),
        P(("dp", "row")),
        P(),
        P("row", "col"),
        P("row", "col"),
        P("row", "col"),
        P("row", "col"),
        P(),
        P(),
        P(),
        P(),
    )
    return jax.shard_map(
        body,
        mesh=mesh,
        in_specs=placed,
        out_specs=(
            P(("dp", "row"), "col", None),
            P(("dp", "row"), "col", None),
            P("row", "col"),
            P("row", "col"),
            P("row", "col"),
            P("row", "col"),
            P(),
            P(),
            P(),
            P(),
        ),
        check_vma=False,
    )
```
